32 devices in a mesh: grp: 2 (over core), gx: 4 (over y, x), gy: 4 (over z).
Axes of the slice: x: 2, y: 2, z: 4, core: 2. Of those that a mesh axis runs over, the one named last changes fastest.
Arguments:
- coarse_density: float32 [512, 512, 512], P('gx', ('grp', 'gy')), may hold values from -3 to 3
- fine_density: float32 [32, 128, 256], P('gx', 'gy', 'grp'), may hold values from -96 to 96
- fine_start: float32 [32, 128, 256], P('gx', 'gy', 'grp'), may hold values from -6 to 6
- anchor: int32 [3], replicated, may hold values from 1 to 447
Outputs:
- coarse_potential: float32 [512, 512, 512], P('gx', ('grp', 'gy'))
- fine_potential: float32 [32, 128, 256], P('gx', 'gy', 'grp')
The draws below stay inside these ranges and needn't reach their ends.
Inputs may be any that keep to these rules, and one draw needn't show every extreme that they name: Along every dimension d the coarse cells anchor[d] - 1 up to anchor[d] + (fine cells along d) / 4 lie inside the coarse grid.
All inputs are finite; a program needn't handle non-finite values.
Results may differ from the reference program's by a relative error of at most 0.00015.
Values sent between devices are 32-bit elements; how exact they have to be, the bound alone decides.
No kernel may reach another device: no remote copies, remote signals or barrier semaphores. Data moves between devices by JAX's collectives and lax.ppermute only.
A program may use at most 128 MiB of HBM per device.

```python
import math
import jax
import jax.numpy as jnp
from jax import lax

NC = 512
RATIO = 4
SWEEPS = 8
FX = 32
FY = 128
FZ = 256
CBX = 10
CBY = 34
CBZ = 66


def block_levels(rng, shape, pieces, low, high):
    def one(dim, parts):
        steps = jax.random.uniform(jax.random.fold_in(jax.random.fold_in(rng, 6), dim), (parts,), jnp.float32, low / len(pieces), high / len(pieces))
        return jnp.repeat(jnp.exp(steps), shape[dim] // parts).reshape((-1,) + (1,) * (len(shape) - dim - 1))

    factor_of = one(*pieces[0])
    for cut in pieces[1:]:
        factor_of = factor_of * one(*cut)
    return factor_of


def gaussian(key, extent, width, reach, cuts=(), kind=jnp.bfloat16):
    values = width * jax.random.normal(key, extent, jnp.float32)
    if cuts:
        values = values * block_levels(key, extent, cuts, -0.22, 0.18)
    return jnp.clip(values, -reach, reach).astype(kind)


def setup_inputs(seed: int = 0) -> dict:
    key_list = jax.random.split(jax.random.key(seed), 5)
    coarse_density = gaussian(key_list[0], (NC, NC, NC), 0.5, 3.0, ((0, 4), (1, 8)), jnp.float32)
    fine_density = gaussian(key_list[1], (FX, FY, FZ), 16.0, 96.0, ((0, 4), (1, 4), (2, 2)), jnp.float32)
    fine_start = gaussian(key_list[2], (FX, FY, FZ), 1.0, 6.0, ((0, 4), (1, 4), (2, 2)), jnp.float32)
    anchor = jax.random.randint(key_list[3], (3,), 1, NC - max(FX, max(FY, FZ)) // RATIO).astype(jnp.int32)
    return dict(coarse_density=coarse_density, fine_density=fine_density, fine_start=fine_start, anchor=anchor)


highest = lax.Precision.HIGHEST

def sine_table(amount):
    indices = jnp.arange(amount, dtype=jnp.int32) + 1
    product = indices[:, None] * indices[None, :] % (2 * (amount + 1))
    angles = product.astype(jnp.float32) * (math.pi / (amount + 1))
    return math.sqrt(2.0 / (amount + 1)) * jnp.sin(angles)

def eigen_values(indices, amount):
    angles = (indices + 1).astype(jnp.float32) * (math.pi / (2 * (amount + 1)))
    return -4.0 * jnp.square(jnp.sin(angles))

def interpolation(fine_index, cell_count):
    scaled = 2 * fine_index + 1 + RATIO
    bottom = scaled // (2 * RATIO)
    weight = (scaled % (2 * RATIO)).astype(jnp.float32) / (2.0 * RATIO)
    column = jnp.arange(cell_count, dtype=jnp.int32)
    first_part = jnp.where(column[None, :] == bottom[:, None], 1.0 - weight[:, None], 0.0)
    second_part = jnp.where(column[None, :] == bottom[:, None] + 1, weight[:, None], 0.0)
    return first_part + second_part

def transform(values, matrix):
    values = jnp.einsum('abc,cd->abd', values, matrix, precision=highest)
    values = jnp.einsum('abc,bd->adc', values, matrix, precision=highest)
    return jnp.einsum('abc,ad->dbc', values, matrix, precision=highest)

def ghost_values(face, left_matrix, right_matrix):
    partial_value = jnp.einsum('fbc,kc->fbk', face, right_matrix, precision=highest)
    return jnp.einsum('fbk,jb->fjk', partial_value, left_matrix, precision=highest)

def reference(coarse_density, fine_density, fine_start, anchor):
    matrix = sine_table(NC)
    eigen_list = eigen_values(jnp.arange(NC, dtype=jnp.int32), NC)
    spectrum = transform(coarse_density, matrix)
    divisor = eigen_list[:, None, None] + eigen_list[None, :, None] + eigen_list[None, None, :]
    potential = transform(spectrum / divisor, matrix)
    coarse_box = lax.dynamic_slice(potential, (anchor[0] - 1, anchor[1] - 1, anchor[2] - 1), (CBX, CBY, CBZ))
    ends_x = interpolation(jnp.array([-1, FX], dtype=jnp.int32), CBX)
    ends_y = interpolation(jnp.array([-1, FY], dtype=jnp.int32), CBY)
    ends_z = interpolation(jnp.array([-1, FZ], dtype=jnp.int32), CBZ)
    inner_x = interpolation(jnp.arange(FX, dtype=jnp.int32), CBX)
    inner_y = interpolation(jnp.arange(FY, dtype=jnp.int32), CBY)
    inner_z = interpolation(jnp.arange(FZ, dtype=jnp.int32), CBZ)
    face_x = jnp.einsum('fa,abc->fbc', ends_x, coarse_box, precision=highest)
    face_y = jnp.einsum('fb,abc->fac', ends_y, coarse_box, precision=highest)
    face_z = jnp.einsum('fc,abc->fab', ends_z, coarse_box, precision=highest)
    ghost_x = ghost_values(face_x, inner_y, inner_z)
    ghost_y = ghost_values(face_y, inner_x, inner_z)
    ghost_z = ghost_values(face_z, inner_x, inner_y)
    padded = jnp.zeros((FX + 2, FY + 2, FZ + 2), jnp.float32)
    padded = padded.at[1:-1, 1:-1, 1:-1].set(fine_start)
    padded = padded.at[0, 1:-1, 1:-1].set(ghost_x[0]).at[-1, 1:-1, 1:-1].set(ghost_x[1])
    padded = padded.at[1:-1, 0, 1:-1].set(ghost_y[0]).at[1:-1, -1, 1:-1].set(ghost_y[1])
    padded = padded.at[1:-1, 1:-1, 0].set(ghost_z[0]).at[1:-1, 1:-1, -1].set(ghost_z[1])
    source = fine_density / (RATIO * RATIO)
    for sweep in range(SWEEPS):
        summed = padded[2:, 1:-1, 1:-1] + padded[:-2, 1:-1, 1:-1]
        summed = summed + padded[1:-1, 2:, 1:-1] + padded[1:-1, :-2, 1:-1]
        summed = summed + padded[1:-1, 1:-1, 2:] + padded[1:-1, 1:-1, :-2]
        padded = padded.at[1:-1, 1:-1, 1:-1].set((summed - source) / 6.0)
    return (potential, padded[1:-1, 1:-1, 1:-1])
```

```python
import math

import jax
import jax.numpy as jnp
from jax import lax
from jax.experimental import pallas as pl
from jax.experimental.pallas import tpu as pltpu
from jax.sharding import PartitionSpec as P

RATIO = 4
SWEEPS = 8


highest = lax.Precision.HIGHEST
high = lax.Precision.HIGH


def sine_table(amount):
    indices = jnp.arange(amount, dtype=jnp.int32) + 1
    product = indices[:, None] * indices[None, :] % (2 * (amount + 1))
    angles = product.astype(jnp.float32) * (math.pi / (amount + 1))
    return math.sqrt(2.0 / (amount + 1)) * jnp.sin(angles)


def eigen_values(indices, amount):
    angles = (indices + 1).astype(jnp.float32) * (math.pi / (2 * (amount + 1)))
    return -4.0 * jnp.square(jnp.sin(angles))


def interpolation(fine_index, cell_count):
    scaled = 2 * fine_index + 1 + RATIO
    bottom = scaled // (2 * RATIO)
    weight = (scaled % (2 * RATIO)).astype(jnp.float32) / (2.0 * RATIO)
    column = jnp.arange(cell_count, dtype=jnp.int32)
    first_part = jnp.where(column[None, :] == bottom[:, None], 1.0 - weight[:, None], 0.0)
    second_part = jnp.where(column[None, :] == bottom[:, None] + 1, weight[:, None], 0.0)
    return first_part + second_part


def ghost_values(face, left_matrix, right_matrix):
    partial_value = jnp.einsum("fbc,kc->fbk", face, right_matrix, precision=highest)
    return jnp.einsum("fbk,jb->fjk", partial_value, left_matrix, precision=highest)


def selection(first_global, length, window_start, window_length):
    here = first_global + jnp.arange(length, dtype=jnp.int32)
    window = window_start + jnp.arange(window_length, dtype=jnp.int32)
    return (here[:, None] == window[None, :]).astype(jnp.float32)


def edge_green(half_squares, length):
    theta = 2.0 * jnp.arcsinh(jnp.sqrt(half_squares))
    bottom = jnp.expm1(-2.0 * (length + 1) * theta)
    near = jnp.exp(-theta) * jnp.expm1(-2.0 * length * theta) / bottom
    far = jnp.exp(-length * theta) * jnp.expm1(-2.0 * theta) / bottom
    return near, far


def couple(first, last, near, far):
    count = len(first)
    kept, slopes, tops, scales = [last[0]], [near], [first[0]], [None]
    for p in range(1, count):
        scale = 1.0 / (1.0 - near * slopes[-1])
        top = (first[p] + near * kept[-1]) * scale
        drop = far * slopes[-1]
        kept_next = last[p] + far * kept[-1] + drop * top
        slopes_next = near + far * drop * scale
        tops.append(top)
        scales.append(scale)
        kept.append(kept_next)
        slopes.append(slopes_next)
    lows = [None] * count
    highs = [None] * count
    zero = jnp.zeros_like(first[0])
    highs[count - 1] = zero
    right = tops[count - 1]
    for p in range(count - 2, -1, -1):
        highs[p] = right
        lows[p + 1] = kept[p] + slopes[p] * right
        if p > 0:
            right = tops[p] + far * scales[p] * right
    lows[0] = zero
    return lows, highs


def with_halo(block, sides, width):
    for axis, dim, fill in sides:
        count = lax.axis_size(axis)
        forward = [(i, i + 1) for i in range(count - 1)]
        backward = [(target, source) for source, target in forward]
        low = lax.ppermute(
            lax.slice_in_dim(block, block.shape[dim] - width, None, axis=dim), axis, forward
        )
        above = lax.ppermute(lax.slice_in_dim(block, 0, width, axis=dim), axis, backward)
        parts = [block, above]
        if fill:
            shape = list(block.shape)
            shape[dim] = fill
            parts.append(jnp.zeros(shape, block.dtype))
        block = jnp.concatenate(parts + [low], axis=dim)
    return block


def halo_index(start, own, fill, width):
    own_part = start + jnp.arange(own + width, dtype=jnp.int32)
    fill_part = jnp.full((fill,), -(RATIO * RATIO * RATIO) - width, jnp.int32)
    low_part = start - width + jnp.arange(width, dtype=jnp.int32)
    return jnp.concatenate([own_part, fill_part, low_part])


def sweeps_kernel(start_ref, source_ref, inside_ref, out_ref, a_ref, b_ref):
    rows, cols, depth = start_ref.shape
    own_rows, own_cols, own_depth = out_ref.shape

    def sweep(src, dst):
        for i in range(rows):
            here = src[i]
            total = src[(i + 1) % rows] + src[(i - 1) % rows]
            total = total + pltpu.roll(here, 1, 0) + pltpu.roll(here, cols - 1, 0)
            total = total + pltpu.roll(here, 1, 1) + pltpu.roll(here, depth - 1, 1)
            dst[i] = (total + source_ref[i]) * inside_ref[i]

    a_ref[...] = start_ref[...]

    def pair(_, carry):
        sweep(a_ref, b_ref)
        sweep(b_ref, a_ref)
        return carry

    lax.fori_loop(0, SWEEPS // 2, pair, 0)
    out_ref[...] = a_ref[:own_rows, :own_cols, :own_depth]


def body(coarse_density, fine_density, fine_start, anchor):
    coarse_rows, coarse_cols, cell_count = coarse_density.shape
    count_x = lax.axis_size("gx")
    count_y = lax.axis_size("grp") * lax.axis_size("gy")
    devices = count_x * count_y
    everyone = ("gx", "grp", "gy")

    fine_rows, fine_cols, fine_depth = fine_start.shape
    total_x = fine_rows * lax.axis_size("gx")
    total_y = fine_cols * lax.axis_size("gy")
    total_z = fine_depth * lax.axis_size("grp")
    width = SWEEPS
    fill = -(fine_depth + 2 * width) % 128
    fine_pair = with_halo(
        jnp.stack([fine_start, fine_density]),
        (("grp", 3, fill), ("gx", 1, 0), ("gy", 2, 0)),
        width,
    )

    matrix_x = sine_table(coarse_rows)
    matrix_y = sine_table(coarse_cols)
    matrix_z = sine_table(cell_count)
    lam_x = eigen_values(jnp.arange(coarse_rows, dtype=jnp.int32), coarse_rows)
    lam_y = eigen_values(jnp.arange(coarse_cols, dtype=jnp.int32), coarse_cols)
    lam_z = eigen_values(jnp.arange(cell_count, dtype=jnp.int32), cell_count)
    divisor = lam_x[:, None, None] + lam_y[None, :, None] + lam_z[None, None, :]

    spectrum = jnp.einsum("abc,cd->abd", coarse_density, matrix_z, precision=high)
    spectrum = jnp.einsum("abc,bd->adc", spectrum, matrix_y, precision=high)
    spectrum = jnp.einsum("abc,ad->dbc", spectrum, matrix_x, precision=high)

    edge_x = (matrix_x[0][:, None, None], matrix_x[coarse_rows - 1][:, None, None])
    edge_y = (matrix_y[0][None, :, None], matrix_y[coarse_cols - 1][None, :, None])
    half_yz = -0.25 * (lam_y[:, None] + lam_z[None, :])
    near_x, far_x = edge_green(half_yz, coarse_rows)
    here_x = lax.axis_index("gx")

    def ghosts_x(edges):
        every = lax.all_gather(edges, "gx", axis=0)
        lows, highs = couple(
            [every[p, 0] for p in range(count_x)],
            [every[p, 1] for p in range(count_x)],
            near_x,
            far_x,
        )
        low, above = lows[0], highs[0]
        for p in range(1, count_x):
            low = jnp.where(here_x == p, lows[p], low)
            above = jnp.where(here_x == p, highs[p], above)
        return low, above

    alone = spectrum / divisor
    low_x, above_x = ghosts_x(
        jnp.stack([jnp.sum(alone * edge_x[0], axis=0), jnp.sum(alone * edge_x[1], axis=0)])
    )
    slab = (spectrum - edge_x[0] * low_x[None] - edge_x[1] * above_x[None]) / divisor
    edges = jnp.stack([jnp.sum(slab * edge_y[0], axis=1), jnp.sum(slab * edge_y[1], axis=1)])
    edges = jnp.einsum("fqk,qx->fkx", edges, matrix_x, precision=highest)
    chunk = cell_count // devices
    edges = edges.reshape(2, devices, chunk, coarse_rows).transpose(1, 0, 2, 3)
    edges = edges.reshape(devices, 2 * chunk, coarse_rows)
    edges = lax.all_to_all(edges, everyone, split_axis=0, concat_axis=0, tiled=True)
    edges = edges.reshape(count_x, count_y, 2 * chunk, coarse_rows).transpose(1, 2, 0, 3)
    edges = edges.reshape(count_y, 2 * chunk, cell_count)
    edges = jnp.einsum("pkx,xq->pkq", edges, matrix_z, precision=highest)
    mine = lax.axis_index(everyone) * chunk + jnp.arange(chunk, dtype=jnp.int32)
    half_zx = -0.25 * (eigen_values(mine, cell_count)[:, None] + lam_z[None, :])
    near_y, far_y = edge_green(half_zx, coarse_cols)
    lows, highs = couple(
        [edges[p, :chunk] for p in range(count_y)],
        [edges[p, chunk:] for p in range(count_y)],
        near_y,
        far_y,
    )
    planes = jnp.stack([jnp.concatenate(both, axis=0) for both in zip(lows, highs)])
    planes = jnp.einsum("pkq,qx->pkx", planes, matrix_z, precision=highest)
    planes = planes.reshape(count_y, 2 * chunk, count_x, coarse_rows).transpose(2, 0, 1, 3)
    planes = planes.reshape(devices, 2 * chunk, coarse_rows)
    planes = lax.all_to_all(planes, everyone, split_axis=0, concat_axis=0, tiled=True)
    planes = planes.reshape(devices, 2, chunk, coarse_rows).transpose(1, 0, 2, 3)
    planes = planes.reshape(2, cell_count, coarse_rows)
    planes = jnp.einsum("fkx,xq->fqk", planes, matrix_x, precision=highest)
    low_y, above_y = planes[0][:, None, :], planes[1][:, None, :]

    side = -(edge_y[0] * low_y + edge_y[1] * above_y)
    added = side / divisor
    more_low, more_above = ghosts_x(
        jnp.stack([jnp.sum(added * edge_x[0], axis=0), jnp.sum(added * edge_x[1], axis=0)])
    )
    low_x = (low_x + more_low)[None]
    above_x = (above_x + more_above)[None]
    spectrum = (spectrum + side - edge_x[0] * low_x - edge_x[1] * above_x) / divisor
    spectrum = jnp.einsum("abc,ad->dbc", spectrum, matrix_x, precision=high)
    spectrum = jnp.einsum("abc,bd->adc", spectrum, matrix_y, precision=high)
    potential = jnp.einsum("abc,cd->abd", spectrum, matrix_z, precision=high)

    bound_x = total_x // RATIO + 2
    bound_y = total_y // RATIO + 2
    bound_z = total_z // RATIO + 2
    coarse_x_start = lax.axis_index("gx") * coarse_rows
    coarse_y_start = lax.axis_index(("grp", "gy")) * coarse_cols
    pick_x = selection(coarse_x_start, coarse_rows, anchor[0] - 1, bound_x)
    pick_y = selection(coarse_y_start, coarse_cols, anchor[1] - 1, bound_y)
    pick_z = selection(0, cell_count, anchor[2] - 1, bound_z)

    def face(dim, total, first):
        faces = []
        for fine_index in (-1, total):
            scaled = 2 * fine_index + 1 + RATIO
            bottom = scaled // (2 * RATIO)
            weight = (scaled % (2 * RATIO)) / (2.0 * RATIO)
            value = 0.0
            for step, part in ((0, 1.0 - weight), (1, weight)):
                place = anchor[dim] - 1 + bottom + step - first
                held = (place >= 0) & (place < potential.shape[dim])
                plane = lax.dynamic_index_in_dim(
                    potential, jnp.clip(place, 0, potential.shape[dim] - 1), dim, keepdims=False
                )
                value = value + jnp.where(held, part, 0.0) * plane
            faces.append(value)
        return jnp.stack(faces)

    ends_z = interpolation(jnp.array([-1, total_z], dtype=jnp.int32), bound_z)
    weight_z = jnp.dot(ends_z, pick_z.T, precision=highest)
    partial_x = jnp.einsum("fyz,yb->fbz", face(0, total_x, coarse_x_start), pick_y, precision=highest)
    partial_y = jnp.einsum("fxz,xa->faz", face(1, total_y, coarse_y_start), pick_x, precision=highest)
    partial_z = jnp.stack([jnp.sum(potential * weight_z[f], axis=2) for f in range(2)])
    partial_z = jnp.einsum("fxy,xa->fay", partial_z, pick_x, precision=highest)
    window_x = jnp.einsum("fbz,zc->fbc", partial_x, pick_z, precision=highest)
    window_y = jnp.einsum("faz,zc->fac", partial_y, pick_z, precision=highest)
    window_z = jnp.einsum("fay,yb->fab", partial_z, pick_y, precision=highest)
    sizes = [window_x.size, window_y.size, window_z.size]
    flat = jnp.concatenate([window_x.ravel(), window_y.ravel(), window_z.ravel()])
    flat = lax.psum(flat, ("grp", "gx", "gy"))
    face_x = flat[: sizes[0]].reshape(window_x.shape)
    face_y = flat[sizes[0] : sizes[0] + sizes[1]].reshape(window_y.shape)
    face_z = flat[sizes[0] + sizes[1] :].reshape(window_z.shape)

    index_x = halo_index(lax.axis_index("gx") * fine_rows, fine_rows, 0, width)
    index_y = halo_index(lax.axis_index("gy") * fine_cols, fine_cols, 0, width)
    index_z = halo_index(lax.axis_index("grp") * fine_depth, fine_depth, fill, width)
    inner_x = interpolation(index_x, bound_x)
    inner_y = interpolation(index_y, bound_y)
    inner_z = interpolation(index_z, bound_z)
    ghost_x = ghost_values(face_x, inner_y, inner_z)
    ghost_y = ghost_values(face_y, inner_x, inner_z)
    ghost_z = ghost_values(face_z, inner_x, inner_y)
    boundary = jnp.where((index_x == 0)[:, None, None], ghost_x[0][None], 0.0)
    boundary = boundary + jnp.where((index_x == total_x - 1)[:, None, None], ghost_x[1][None], 0.0)
    boundary = boundary + jnp.where((index_y == 0)[None, :, None], ghost_y[0][:, None, :], 0.0)
    boundary = boundary + jnp.where(
        (index_y == total_y - 1)[None, :, None], ghost_y[1][:, None, :], 0.0
    )
    boundary = boundary + jnp.where((index_z == 0)[None, None, :], ghost_z[0][:, :, None], 0.0)
    boundary = boundary + jnp.where(
        (index_z == total_z - 1)[None, None, :], ghost_z[1][:, :, None], 0.0
    )
    inside_x = (index_x >= 0) & (index_x < total_x)
    inside_y = (index_y >= 0) & (index_y < total_y)
    inside_z = (index_z >= 0) & (index_z < total_z)
    inside = inside_x[:, None, None] & inside_y[None, :, None] & inside_z[None, None, :]
    source = boundary - fine_pair[1] / (RATIO * RATIO)
    shape = fine_pair.shape[1:]
    values = pl.pallas_call(
        sweeps_kernel,
        out_shape=jax.ShapeDtypeStruct(fine_start.shape, fine_start.dtype),
        scratch_shapes=[pltpu.VMEM(shape, jnp.float32), pltpu.VMEM(shape, jnp.float32)],
        name="sweeps",
    )(fine_pair[0], source, jnp.where(inside, 1.0 / 6.0, 0.0))
    return (potential, values)


def solution(mesh):
    return jax.shard_map(
        body,
        mesh=mesh,
        in_specs=(P("gx", ("grp", "gy"), None), P("gx", "gy", "grp"), P("gx", "gy", "grp"), P()),
        out_specs=(P("gx", ("grp", "gy"), None), P("gx", "gy", "grp")),
        check_vma=False,
    )
```
